32 devices in a mesh: stretch: 8 (over y, x, core), head: 4 (over z).
Axes of the slice: x: 2, y: 2, z: 4, core: 2. Of those that a mesh axis runs over, the one named last changes fastest.
Arguments:
- q_items: bfloat16 [8, 432, 32, 128], P('stretch', None, 'head'), may hold values from -6 to 6
- k_items: bfloat16 [8, 432, 8, 128], P('stretch', None, 'head'), may hold values from -6 to 6
- v_items: bfloat16 [8, 432, 8, 128], P('stretch', None, 'head'), may hold values from -6 to 6
- d_out: bfloat16 [8, 432, 32, 128], P('stretch', None, 'head'), may hold values from -6 to 6
- reader_query: float32 [1024, 32, 128], P('stretch', 'head'), may hold values from -6 to 6
- reader_span: int32 [1024], P('stretch'), may hold values from 1 to 8
- target: float32 [1024, 4096], P('stretch', 'head'), may hold values from -6 to 6
- out_proj: float32 [4096, 4096], P('stretch', 'head'), may hold values from -0.09375 to 0.09375
Outputs:
- q_items_grad: float32 [8, 432, 32, 128], P('stretch', None, 'head')
- k_items_grad: float32 [8, 432, 8, 128], P('stretch', None, 'head')
- v_items_grad: float32 [8, 432, 8, 128], P('stretch', None, 'head')
- reader_query_grad: float32 [1024, 32, 128], P('stretch', 'head')
- out_proj_grad: float32 [4096, 4096], P('stretch', 'head')
The draws below stay inside these ranges and needn't reach their ends.
All inputs are finite; a program needn't handle non-finite values.
Results may differ from the reference program's by a relative error of at most 0.0093.
Values may be sent and summed in bfloat16 or wider, within the bound.
A program may use at most 128 MiB of HBM per device.

```python
import jax
import jax.numpy as jnp
from jax import lax

D = 4096
QUERY_HEADS = 32
KV_HEADS = 8
HEAD_DIM = 128
SEG_LEN = 384
BEACONS = 48
SEGMENTS = 8
READERS = 1024


def base_values(key, shape):
    return jnp.clip(jax.random.normal(key, shape, jnp.float32), -4.0, 4.0)


def draw_k_items(key, part):
    shape = (SEGMENTS, SEG_LEN + BEACONS, KV_HEADS, HEAD_DIM)
    drawn = base_values(jax.random.fold_in(key, 1), shape)
    return drawn.astype(jnp.bfloat16)


def draw_q_items(key, part):
    shape = (SEGMENTS, SEG_LEN + BEACONS, QUERY_HEADS, HEAD_DIM)
    drawn = base_values(jax.random.fold_in(key, 2), shape)
    return drawn.astype(jnp.bfloat16)


def draw_reader_query(key, part):
    shape = (READERS, QUERY_HEADS, HEAD_DIM)
    drawn = base_values(jax.random.fold_in(key, 3), shape)
    return drawn


def place_ends(values, stream_key, smallest, top_value):
    place = [jax.random.randint(jax.random.fold_in(stream_key, axis), (), 0, length) for axis, length in enumerate(values.shape)]
    longest = values.shape.index(max(values.shape))
    beside = place[:longest] + [(place[longest] + 1) % values.shape[longest]] + place[longest + 1:]
    return values.at[tuple(place)].set(smallest).at[tuple(beside)].set(top_value)


def levels(key, dims, shards, least, largest):
    loudness = 1.0
    for axis_at, shards_of in shards:
        heights = jax.random.uniform(jax.random.fold_in(jax.random.fold_in(key, 6), axis_at), (shards_of,), jnp.float32, least / len(shards), largest / len(shards))
        loudness = loudness * jnp.repeat(jnp.exp(heights), dims[axis_at] // shards_of).reshape((-1,) + (1,) * (len(dims) - 1 - axis_at))
    return loudness


def noise(own_key, extent, width, reach, split=(), kind=jnp.bfloat16):
    array = jax.random.normal(own_key, extent, jnp.float32) * width
    if len(split) > 0:
        array = levels(own_key, extent, split, -0.22, 0.18) * array
    return jnp.clip(array, min=-reach, max=reach).astype(kind)


def setup_inputs(seed: int = 0) -> dict:
    key_list = jax.random.split(jax.random.key(seed), 9)
    q_items = draw_q_items(jax.random.fold_in(key_list[8], 71), 0)
    k_items = draw_k_items(jax.random.fold_in(key_list[8], 71), 0)
    v_items = noise(key_list[2], (SEGMENTS, SEG_LEN + BEACONS, KV_HEADS, HEAD_DIM), 1.0, 6.0, ((0, 8), (2, 4)))
    d_out = noise(key_list[3], (SEGMENTS, SEG_LEN + BEACONS, QUERY_HEADS, HEAD_DIM), 1.0, 6.0, ((0, 8), (2, 4)))
    reader_query = draw_reader_query(jax.random.fold_in(key_list[8], 71), 0)
    reader_span = place_ends(jax.random.randint(key_list[5], (READERS,), 1, SEGMENTS + 1), jax.random.fold_in(key_list[5], 1), 1, SEGMENTS).astype(jnp.int32)
    target = noise(key_list[6], (READERS, D), 1.0, 6.0, ((0, 8), (1, 4)), jnp.float32)
    out_proj = noise(key_list[7], (D, D), D ** -0.5, 0.09375, ((0, 8), (1, 4)), jnp.float32)
    return {"q_items": q_items, "k_items": k_items, "v_items": v_items, "d_out": d_out, "reader_query": reader_query, "reader_span": reader_span, "target": target, "out_proj": out_proj}


def product(pattern, former, latter):
    return jnp.einsum(pattern, former.astype(jnp.float32), latter.astype(jnp.float32), precision=lax.Precision.HIGHEST)


def narrowed(values):
    return lax.optimization_barrier(values.astype(jnp.bfloat16))


def softmax_rows(scores, visible):
    masked = jnp.where(visible, scores, -1e30)
    row_top = jnp.max(masked, axis=-1, keepdims=True)
    raised = jnp.where(visible, jnp.exp(masked - row_top), 0.0)
    return raised / jnp.sum(raised, axis=-1, keepdims=True)


def segment_grads(block_index, q_block, k_block, v_block, d_block, beacon_k, beacon_v, key_block):
    item_count, query_heads, head_width = q_block.shape
    groups = k_block.shape[1]
    per_group = query_heads // groups
    scaling = head_width ** -0.5
    beacon_count = beacon_k.shape[0]
    all_keys = jnp.concatenate([beacon_k, k_block], axis=0)
    all_values = jnp.concatenate([beacon_v, v_block], axis=0)
    queries = q_block.reshape(item_count, groups, per_group, head_width)
    out_grads = d_block.reshape(item_count, groups, per_group, head_width)
    causal = jnp.arange(item_count)[:, None] >= jnp.arange(item_count)[None, :]
    earlier = jnp.broadcast_to((key_block < block_index)[None, :], (item_count, beacon_count))
    visible = jnp.concatenate([earlier, causal], axis=1)
    scores = product("sgah,kgh->gask", queries, all_keys) * scaling
    probs = softmax_rows(scores, visible)
    prob_grad = product("sgah,kgh->gask", out_grads, all_values)
    row_total = jnp.sum(probs * prob_grad, axis=-1, keepdims=True)
    score_grad = narrowed(probs * (prob_grad - row_total) * scaling)
    rounded = narrowed(probs)
    q_grad = product("gask,kgh->sgah", score_grad, all_keys).reshape(item_count, query_heads, head_width)
    k_grad = product("gask,sgah->kgh", score_grad, queries)
    v_grad = product("gask,sgah->kgh", rounded, out_grads)
    return q_grad, k_grad[beacon_count:], v_grad[beacon_count:], k_grad[:beacon_count], v_grad[:beacon_count]


def reference(q_items, k_items, v_items, d_out, reader_query, reader_span, target, out_proj):
    per_group = QUERY_HEADS // KV_HEADS
    scaling = HEAD_DIM ** -0.5
    beacon_total = SEGMENTS * BEACONS
    beacon_k = k_items[:, SEG_LEN:].reshape(beacon_total, KV_HEADS, HEAD_DIM)
    beacon_v = v_items[:, SEG_LEN:].reshape(beacon_total, KV_HEADS, HEAD_DIM)
    key_block = (jnp.arange(beacon_total) // BEACONS).astype(jnp.int32)

    def advance(carry, inputs):
        block_index, q_block, k_block, v_block, d_block = inputs
        q_grad, k_own, v_own, k_far, v_far = segment_grads(block_index, q_block, k_block, v_block, d_block, beacon_k, beacon_v, key_block)
        return (carry[0] + k_far, carry[1] + v_far), (q_grad, k_own, v_own)

    empty = jnp.zeros((beacon_total, KV_HEADS, HEAD_DIM), jnp.float32)
    (token_dk, token_dv), (q_grads, k_grads, v_grads) = lax.scan(
        advance, (empty, empty), (jnp.arange(SEGMENTS).astype(jnp.int32), q_items, k_items, v_items, d_out))

    wide_k = beacon_k.astype(jnp.float32)
    wide_v = beacon_v.astype(jnp.float32)
    queries = reader_query.reshape(READERS, KV_HEADS, per_group, HEAD_DIM)
    visible = key_block[None, :] < reader_span[:, None]
    scores = product("rgah,kgh->gark", queries, wide_k) * scaling
    probs = softmax_rows(scores, visible)
    attended = product("gark,kgh->rgah", probs, wide_v).reshape(READERS, D)
    errors = jnp.dot(attended, out_proj.T, precision=lax.Precision.HIGHEST) - target
    out_proj_grad = jnp.dot(errors.T, attended, precision=lax.Precision.HIGHEST)
    attended_grad = jnp.dot(errors, out_proj, precision=lax.Precision.HIGHEST).reshape(READERS, KV_HEADS, per_group, HEAD_DIM)
    prob_grad = product("rgah,kgh->gark", attended_grad, wide_v)
    row_total = jnp.sum(probs * prob_grad, axis=-1, keepdims=True)
    score_grad = probs * (prob_grad - row_total) * scaling
    reader_query_grad = product("gark,kgh->rgah", score_grad, wide_k).reshape(READERS, QUERY_HEADS, HEAD_DIM)
    reader_dk = product("gark,rgah->kgh", score_grad, queries)
    reader_dv = product("gark,rgah->kgh", probs, attended_grad)

    beacon_dk = (token_dk + reader_dk).reshape(SEGMENTS, BEACONS, KV_HEADS, HEAD_DIM)
    beacon_dv = (token_dv + reader_dv).reshape(SEGMENTS, BEACONS, KV_HEADS, HEAD_DIM)
    k_items_grad = k_grads.at[:, SEG_LEN:].add(beacon_dk)
    v_items_grad = v_grads.at[:, SEG_LEN:].add(beacon_dv)
    return q_grads, k_items_grad, v_items_grad, reader_query_grad, out_proj_grad
```

```python
import contextlib
import functools

import jax
import jax.numpy as jnp
from jax import lax
from jax.experimental import pallas as pl
from jax.experimental.pallas import tpu as pltpu
from jax.sharding import PartitionSpec as P

SEG_LEN = 384
MESH = pl.DeviceIdType.MESH
F32 = jnp.float32
BF16 = jnp.bfloat16
ROWS = 256
BLOCKED = -1e30
LAG = 2
PIECES = 2


def dot(former, latter, left=1, right=0):
    return lax.dot_general(
        former, latter, (((left,), (right,)), ((), ())), preferred_element_type=F32
    )


def phase(name):
    return contextlib.nullcontext()


def fused(n, heads_axis, *refs):
    (q_ref, d_ref, k_ref, v_ref, kvb_ref, rq_ref, span_ref, tgt_ref, w_ref,
     qg_ref, kg_ref, vg_ref, rqg_ref, opg_ref,
     tb, tgt_in, wb, kv_all, ak, av, akt, bias, dk, dv, probs,
     att_own, att_all, part, rin, lin, rout, lout, err_all, gsend, pin, gout, gin, acc,
     far, fin,
     tgt_s, tgt_r, kv_s, kv_r, att_s, att_f, att_r, ro_s, rin_r, lo_s, lin_r,
     gs_s, gs_r, go_s, go_r, far_s, far_r) = refs
    s = lax.axis_index("stretch")
    h = lax.axis_index("head")
    q = n // heads_axis
    last = heads_axis - 1
    query_heads, items, width = q_ref.shape
    groups = k_ref.shape[0]
    per_group = query_heads // groups
    beacons = kvb_ref.shape[2]
    far_total = n * beacons
    readers, features = att_own.shape
    outs = wb.shape[0]
    scaling = width ** (-0.5)
    pending = []

    def remote(src, dst, send_sem, recv_sem, device):
        return pltpu.make_async_remote_copy(
            src_ref=src, dst_ref=dst, send_sem=send_sem, recv_sem=recv_sem,
            device_id=device, device_id_type=MESH,
        )

    def send(src, dst, send_sem, recv_sem, device, own=None):
        copy = remote(src, dst, send_sem, recv_sem, device)
        if own is None:
            copy.start()
            pending.append(copy.wait_send)
            return

        @pl.when(jnp.logical_not(own))
        def _():
            copy.start()

        @pl.when(own)
        def _():
            pltpu.make_async_copy(src, dst, recv_sem).start()

        def finish():
            @pl.when(jnp.logical_not(own))
            def _():
                copy.wait_send()

        pending.append(finish)

    def landed(dst, sem):
        pltpu.make_async_copy(dst, dst, sem).wait()

    with phase("barrier"):
        for j in range(q):
            tb[j] = tgt_ref[:, j * outs:(j + 1) * outs].astype(BF16)

        barrier = pltpu.get_barrier_semaphore()
        for k in range(1, n):
            pl.semaphore_signal(barrier, inc=1, device_id=(s ^ k, h), device_id_type=MESH)

        @pl.when(h > 0)
        def _():
            pl.semaphore_signal(barrier, inc=1, device_id=(s, h - 1), device_id_type=MESH)

        @pl.when(h < last)
        def _():
            pl.semaphore_signal(barrier, inc=1, device_id=(s, h + 1), device_id_type=MESH)

        beside = jnp.where(h > 0, 1, 0) + jnp.where(h < last, 1, 0)
        pl.semaphore_wait(barrier, n - 1 + beside)

    with phase("setup"):
        for k in range(1, n):
            send(kvb_ref, kv_all.at[s], kv_s.at[k], kv_r.at[s], (s ^ k, h))
        pltpu.make_async_copy(kvb_ref, kv_all.at[s], kv_r.at[s]).start()
        for j in range(q):
            column = h * q + j
            send(tb.at[j], tgt_in.at[s], tgt_s.at[j], tgt_r.at[s], (column, h), column == s)

        wb[...] = w_ref[...].astype(BF16)
        keys = far_total + items
        key_at = lax.broadcasted_iota(jnp.int32, (keys, items), 0)
        row_at = lax.broadcasted_iota(jnp.int32, (keys, items), 1)
        margin = jnp.where(key_at < far_total, s * beacons - 1 - key_at, row_at + far_total - key_at)
        bias[...] = jnp.where(margin >= 0, 0.0, BLOCKED).astype(F32)
        dk[...] = jnp.zeros_like(dk)
        dv[...] = jnp.zeros_like(dv)

        @pl.when(h == 0)
        def _():
            rin[...] = jnp.zeros_like(rin)

        @pl.when(h == last)
        def _():
            lin[...] = jnp.zeros_like(lin)

        for g in range(groups):
            ak[g, far_total:] = k_ref[g]
            av[g, far_total:] = v_ref[g]

    with phase("kvwait"):
        for k in range(n):
            landed(kv_all.at[s ^ k], kv_r.at[s ^ k])
        for g in range(groups):
            for b in range(n):
                ak[g, b * beacons:(b + 1) * beacons] = kv_all[b, 0, g]
                av[g, b * beacons:(b + 1) * beacons] = kv_all[b, 1, g]
            akt[g] = ak[g].astype(F32).T.astype(BF16)

    spans = span_ref[...] * beacons
    hidden = lax.broadcasted_iota(jnp.int32, (far_total, readers), 0) >= spans

    def lanes(head):
        return pl.ds(pl.multiple_of(head * width, width), width)

    def read_head(head, carry):
        g = head // per_group
        query = rq_ref[:, lanes(head)]
        high = query.astype(BF16)
        low = (query - high.astype(F32)).astype(BF16)
        keyed = ak[g, :far_total]
        scores = (dot(keyed, high, 1, 1) + dot(keyed, low, 1, 1)) * scaling
        scores = jnp.where(hidden, BLOCKED, scores)
        raised = jnp.exp(scores - jnp.max(scores, axis=0, keepdims=True))
        normal = raised / jnp.sum(raised, axis=0, keepdims=True)
        probs[head] = normal
        found = dot(normal.astype(BF16), av[g, :far_total], 0, 0)
        att_own[:, lanes(head)] = found.astype(BF16)
        return carry

    with phase("read"):
        lax.fori_loop(0, query_heads, read_head, 0)

        for k in [1] + list(range(2, n, 2)):
            send(att_own, att_all.at[s], att_s.at[k], att_r.at[s], (s ^ k, h))
        pltpu.make_async_copy(att_own, att_all.at[s], att_r.at[s]).start()

    def segment_head(head, carry):
        g = head // per_group
        for start in range(0, items, ROWS):
            stop = min(start + ROWS, items)
            reach = far_total + stop
            query = q_ref[head, start:stop]
            grad = d_ref[head, start:stop]
            scores = dot(ak[g, :reach], query, 1, 1) * scaling + bias[:reach, start:stop]
            raised = jnp.exp(scores - jnp.max(scores, axis=0, keepdims=True))
            normal = raised * (1.0 / jnp.sum(raised, axis=0, keepdims=True))
            prob_grad = dot(av[g, :reach], grad, 1, 1)
            total = jnp.sum(normal * prob_grad, axis=0, keepdims=True)
            score_grad = (normal * (prob_grad - total) * scaling).astype(BF16)
            dv[g, :reach] += dot(normal.astype(BF16), grad)
            dk[g, :reach] += dot(score_grad, query)
            qg_ref[head, start:stop] = dot(akt[g, :, :reach], score_grad).T
        return carry

    half = readers // PIECES
    steps = n + LAG * last

    def onward(at, came, came_r, out, out_s, has, more, device):
        @pl.when(jnp.logical_and(at >= 0, at < n))
        def _():
            for c in range(PIECES):
                rows = pl.ds(c * half, half)

                @pl.when(has)
                def _():
                    landed(came.at[at, rows], came_r.at[at, c])

                @pl.when(more)
                def _():
                    out[at, rows] = (part[at, rows] + came[at, rows].astype(F32)).astype(BF16)
                    remote(out.at[at, rows], came.at[at, rows], out_s.at[at, c], came_r.at[at, c], device).start()

    right = (s, jnp.minimum(h + 1, last))
    left = (s, jnp.maximum(h - 1, 0))

    def step(t, carry):
        with phase("part"):
            @pl.when(t < n)
            def _():
                block = s ^ t
                landed(att_all.at[block], att_r.at[block])

                @pl.when(jnp.logical_and(t % 2 == 0, t > 0))
                def _():
                    remote(att_all.at[block], att_all.at[block], att_f.at[t], att_r.at[block], (s ^ 1, h)).start()

                part[t] = dot(att_all[block], wb[...], 1, 1)

                @pl.when(s // q == h)
                def _():
                    landed(tgt_in.at[block], tgt_r.at[block])
                    part[t] = part[t] - tgt_in[block].astype(F32)

        with phase("onward"):
            onward(t - LAG * h, rin, rin_r, rout, ro_s, h > 0, h < last, right)
            onward(t - LAG * (last - h), lin, lin_r, lout, lo_s, h < last, h > 0, left)

        with phase("grad"):
            e = t - LAG * last

            @pl.when(e >= 0)
            def _():
                block = s ^ e
                m = e // 2
                found = part[e] + rin[e].astype(F32) + lin[e].astype(F32)
                err_all[block] = found.astype(BF16)

                @pl.when(e % 2 == 0)
                def _():
                    gsend[m] = dot(err_all[block], wb[...]).astype(BF16)
                    remote(gsend.at[m], pin.at[m], gs_s.at[m], gs_r.at[m], (s ^ 1, h)).start()

                @pl.when(e % 2 == 1)
                def _():
                    mine = dot(err_all[block], wb[...])
                    landed(pin.at[m], gs_r.at[m])
                    gout[m] = (mine + pin[m].astype(F32)).astype(BF16)
                    remote(gout.at[m], gin.at[m], go_s.at[m], go_r.at[m], (block, h)).start()

        with phase("segment"):
            lax.fori_loop(t * query_heads // steps, (t + 1) * query_heads // steps, segment_head, 0)
        return carry

    lax.fori_loop(0, steps, step, 0)

    flat_err = err_all.reshape(n * readers, outs)
    flat_att = att_all.reshape(n * readers, features)

    def weight_rows(step, carry):
        at = pl.multiple_of(step * 128, 128)
        opg_ref[pl.ds(at, 128), :] = dot(flat_err[:, pl.ds(at, 128)], flat_att[...], 0, 0)
        return carry

    with phase("weight"):
        lax.fori_loop(0, outs // 128, weight_rows, 0)

    with phase("ginwait"):
        for m in range(n // 2):
            landed(gin.at[m], go_r.at[m])
        total = gin[0].astype(F32)
        for m in range(1, n // 2):
            total += gin[m].astype(F32)
        acc[...] = total

    def read_grad(head, carry):
        g = head // per_group
        grad = acc[:, lanes(head)].astype(BF16)
        normal = probs[head]
        prob_grad = dot(av[g, :far_total], grad, 1, 1)
        total = jnp.sum(normal * prob_grad, axis=0, keepdims=True)
        score_grad = (normal * (prob_grad - total) * scaling).astype(BF16)
        dv[g, :far_total] += dot(normal.astype(BF16), grad)
        dk[g, :far_total] += dot(score_grad, rq_ref[:, lanes(head)].astype(BF16))
        rqg_ref[:, lanes(head)] = dot(akt[g, :, :far_total], score_grad).T
        return carry

    with phase("readgrad"):
        lax.fori_loop(0, query_heads, read_grad, 0)

    with phase("far"):
        for b in range(n):
            for g in range(groups):
                far[b, 0, g] = dk[g, b * beacons:(b + 1) * beacons].astype(BF16)
                far[b, 1, g] = dv[g, b * beacons:(b + 1) * beacons].astype(BF16)
        for k in range(1, n):
            send(far.at[s ^ k], fin.at[k], far_s.at[k], far_r.at[k], (s ^ k, h))
        for g in range(groups):
            kg_ref[g] = dk[g, far_total:]
            vg_ref[g] = dv[g, far_total:]
        start = items - beacons
        mine_at = pl.ds(pl.multiple_of(s * beacons, beacons), beacons)
        for g in range(groups):
            kg_ref[g, start:] += dk[g, mine_at]
            vg_ref[g, start:] += dv[g, mine_at]
    with phase("finwait"):
        for k in range(1, n):
            landed(fin.at[k], far_r.at[k])
            for g in range(groups):
                kg_ref[g, start:] += fin[k, 0, g].astype(F32)
                vg_ref[g, start:] += fin[k, 1, g].astype(F32)

    with phase("finish"):
        for finish in pending:
            finish()
        for t in range(2, n, 2):
            landed(att_own, att_f.at[t])
        for m in range(n // 2):
            landed(gsend.at[m], gs_s.at[m])
            landed(gout.at[m], go_s.at[m])

        def sent(out, out_s):
            for t in range(n):
                for c in range(PIECES):
                    landed(out.at[t, pl.ds(c * half, half)], out_s.at[t, c])

        pl.when(h < last)(lambda: sent(rout, ro_s))
        pl.when(h > 0)(lambda: sent(lout, lo_s))


def body(n, heads_axis, q_items, k_items, v_items, d_out, reader_query, reader_span, target, out_proj):
    items, query_heads, width = q_items.shape[1:]
    groups = k_items.shape[2]
    readers = reader_query.shape[0]
    outs, features = out_proj.shape
    beacons = items - SEG_LEN
    q = n // heads_axis
    far_total = n * beacons
    keys = far_total + items
    queries = jnp.transpose(q_items[0], (1, 0, 2))
    grads = jnp.transpose(d_out[0], (1, 0, 2))
    own_k = jnp.transpose(k_items[0], (1, 0, 2))
    own_v = jnp.transpose(v_items[0], (1, 0, 2))
    kvb = jnp.stack([own_k[:, SEG_LEN:], own_v[:, SEG_LEN:]])
    vm = pltpu.VMEM
    dma = pltpu.SemaphoreType.DMA
    half = n // 2
    blocks = (n, readers, outs)
    scratch = [
        vm((q, readers, outs), BF16), vm(blocks, BF16), vm((outs, features), BF16),
        vm((n, 2, groups, beacons, width), BF16),
        vm((groups, keys, width), BF16), vm((groups, keys, width), BF16),
        vm((groups, width, keys), BF16), vm((keys, items), F32),
        vm((groups, keys, width), F32), vm((groups, keys, width), F32),
        vm((query_heads, far_total, readers), F32),
        vm((readers, features), BF16), vm((n, readers, features), BF16),
        vm(blocks, F32), vm(blocks, BF16), vm(blocks, BF16), vm(blocks, BF16), vm(blocks, BF16), vm(blocks, BF16),
        vm((half, readers, features), BF16), vm((half, readers, features), BF16),
        vm((half, readers, features), BF16), vm((half, readers, features), BF16),
        vm((readers, features), F32),
        vm((n, 2, groups, beacons, width), BF16), vm((n, 2, groups, beacons, width), BF16),
        dma((q,)), dma((n,)), dma((n,)), dma((n,)),
        dma((n,)), dma((n,)), dma((n,)),
        dma((n, PIECES)), dma((n, PIECES)), dma((n, PIECES)), dma((n, PIECES)),
        dma((half,)), dma((half,)), dma((half,)), dma((half,)),
        dma((n,)), dma((n,)),
    ]
    space = pl.BlockSpec(memory_space=pltpu.VMEM)
    shape = jax.ShapeDtypeStruct
    qg, kg, vg, rqg, opg = pl.pallas_call(
        functools.partial(fused, n, heads_axis),
        out_shape=(
            shape((query_heads, items, width), F32),
            shape((groups, items, width), F32),
            shape((groups, items, width), F32),
            shape((readers, features), F32),
            shape((outs, features), F32),
        ),
        in_specs=[space] * 9,
        out_specs=(space,) * 5,
        scratch_shapes=scratch,
        compiler_params=pltpu.CompilerParams(
            collective_id=0, has_side_effects=True, vmem_limit_bytes=60 * 1024 * 1024
        ),
    )(
        queries, grads, own_k, own_v, kvb, reader_query.reshape(readers, features),
        reader_span.reshape(1, readers), target, out_proj,
    )
    return (
        jnp.transpose(qg, (1, 0, 2))[None],
        jnp.transpose(kg, (1, 0, 2))[None],
        jnp.transpose(vg, (1, 0, 2))[None],
        rqg.reshape(reader_query.shape),
        opg,
    )


def solution(mesh):
    n = mesh.shape["stretch"]
    heads_axis = mesh.shape["head"]
    return jax.shard_map(
        functools.partial(body, n, heads_axis),
        mesh=mesh,
        in_specs=(
            P("stretch", None, "head", None),
            P("stretch", None, "head", None),
            P("stretch", None, "head", None),
            P("stretch", None, "head", None),
            P("stretch", "head", None),
            P("stretch"),
            P("stretch", "head"),
            P("stretch", "head"),
        ),
        out_specs=(
            P("stretch", None, "head", None),
            P("stretch", None, "head", None),
            P("stretch", None, "head", None),
            P("stretch", "head", None),
            P("stretch", "head"),
        ),
        check_vma=False,
    )
```
